256 devices in a mesh: ctx: 64 (over z, y, core), tp: 4 (over x).
Axes of the slice: x: 4, y: 4, z: 8, core: 2. Of those that a mesh axis runs over, the one named last changes fastest.
Arguments:
- queries: bfloat16 [8192, 8192], P('ctx', 'tp'), may hold values from -6 to 6
- rotated_keys: bfloat16 [8192, 1024], P('ctx', 'tp'), may hold values from -6 to 6
- value_vectors: bfloat16 [8192, 1024], P('ctx', 'tp'), may hold values from -6 to 6
- doc_lengths: int32 [64], replicated, may hold values from 1 to 1024, 8192 in all
- owner_lists: int32 [64, 64], replicated, may hold values from 0 to 63, as said below
- out_weight: bfloat16 [4096, 8192], P('ctx', 'tp'), may hold values from -0.0625 to 0.0625
Outputs:
- layer_out: bfloat16 [8192, 4096], P('ctx', 'tp')
The draws below stay inside these ranges and needn't reach their ends.
Inputs may be any that keep to these rules, and one draw needn't show every extreme that they name: `doc_lengths`: the lengths add up to 8192; the longest is exactly 1024. Each row and each column of owner_lists names every owner index once.
All inputs are finite; a program needn't handle non-finite values.
Results may differ from the reference program's by a relative error of at most 0.015.
Values may be sent and summed in bfloat16 or wider, within the bound.
No kernel may reach another device: no remote copies, remote signals or barrier semaphores. Data moves between devices by JAX's collectives and lax.ppermute only.
A program may use at most 128 MiB of HBM per device.

```python
import math
import jax
import jax.numpy as jnp
import numpy as np
from jax import lax

QUERY_HEAD_COUNT = 64
KEY_VALUE_HEADS = 8
HEAD_SIZE = 128
DW = 4096
PACKED_TOKENS = 8192
G = 2
MAXDOC = 1024
NDOC = 64
N_CTX = 64


def draw_queries(key, part):
    qkey = jax.random.fold_in(key, 101)
    base_offset = jnp.clip(jax.random.normal(qkey, (PACKED_TOKENS, QUERY_HEAD_COUNT * HEAD_SIZE), jnp.float32), -6.0, 6.0)
    return base_offset.astype(jnp.bfloat16)


def draw_rotated_keys(key, part):
    key_seed = jax.random.fold_in(key, 202)
    base_offset = jnp.clip(jax.random.normal(key_seed, (PACKED_TOKENS, KEY_VALUE_HEADS * HEAD_SIZE), jnp.float32), -6.0, 6.0)
    return base_offset.astype(jnp.bfloat16)


def draw_owner_lists(key, part):
    first = jax.random.permutation(jax.random.fold_in(key, 21), N_CTX)
    second = jax.random.permutation(jax.random.fold_in(key, 22), N_CTX)
    relabel = jax.random.permutation(jax.random.fold_in(key, 23), N_CTX)
    return relabel[(first[:, None] + second[None, :]) % N_CTX].astype(jnp.int32)


def level_of(stream_key, dims, shards, least, high):
    factor_of = 1.0
    for axis_at, shards_of in shards:
        draws = jax.random.uniform(jax.random.fold_in(jax.random.fold_in(stream_key, 6), axis_at), (shards_of,), jnp.float32, least / len(shards), high / len(shards))
        factor_of = factor_of * jnp.repeat(jnp.exp(draws), dims[axis_at] // shards_of).reshape((-1,) + (1,) * (len(dims) - 1 - axis_at))
    return factor_of


def profile(count, total, bound, lean):
    loads = [(1 << 20) // math.isqrt(standing ** lean) + 1 for standing in range(2, count + 1)]
    surplus, given = total - bound - (count - 1), [1] * (count - 1)
    while surplus > 0:
        free = [i for i in range(count - 1) if given[i] < bound]
        whole, remaining = sum([loads[i] for i in free]), surplus
        for i in free:
            extra = min(bound - given[i], max(1, remaining * loads[i] // whole), surplus)
            given[i] = given[i] + extra
            surplus = surplus - extra
    return np.array([bound] + given)


def ragged_sizes(key, number_of, total, limit, skew):
    if number_of == 2:
        one = jax.random.randint(key, (), max(1, total - limit), min(limit, total - 1) + 1)
        return jnp.stack([one, total - one])
    tallies = jnp.asarray(profile(number_of, total, limit, skew), jnp.int32)
    pairs = (number_of - 1) // 2
    giver, taker = tallies[1:1 + 2 * pairs:2], tallies[2:2 + 2 * pairs:2]
    slack = jnp.minimum(giver - 1, limit - taker)
    moved = jax.random.randint(jax.random.fold_in(key, 1), (pairs,), 0, 1 << 20) % (slack + 1)
    tallies = tallies.at[1:1 + 2 * pairs:2].set(giver - moved).at[2:2 + 2 * pairs:2].set(taker + moved)
    return tallies[jax.random.permutation(jax.random.fold_in(key, 2), number_of)]


def gaussian(key, extent, width, limit, pieces=(), kind=jnp.bfloat16):
    values = jax.random.normal(key, extent, jnp.float32) * width
    if len(pieces) > 0:
        values = level_of(key, extent, pieces, -0.22, 0.18) * values
    return jnp.clip(values, min=-limit, max=limit).astype(kind)


def setup_inputs(seed: int = 0) -> dict:
    splits = jax.random.split(jax.random.key(seed), 7)
    queries = draw_queries(jax.random.fold_in(splits[6], 71), 0)
    rotated_keys = draw_rotated_keys(jax.random.fold_in(splits[6], 71), 0)
    value_vectors = gaussian(splits[2], (PACKED_TOKENS, KEY_VALUE_HEADS * HEAD_SIZE), 1.0, 6.0, ((0, 64), (1, 4)))
    doc_lengths = ragged_sizes(splits[3], NDOC, PACKED_TOKENS, MAXDOC, 2).astype(jnp.int32)
    owner_lists = draw_owner_lists(jax.random.fold_in(splits[6], 71), 0)
    out_weight = gaussian(splits[5], (DW, QUERY_HEAD_COUNT * HEAD_SIZE), (QUERY_HEAD_COUNT * HEAD_SIZE) ** -0.5, 0.0625, ((0, 64), (1, 4)))
    return {"queries": queries, "rotated_keys": rotated_keys, "value_vectors": value_vectors, "doc_lengths": doc_lengths, "owner_lists": owner_lists, "out_weight": out_weight}


negative_fill = -1e+30

def doc_index(doc_ends, positions):
    return lax.optimization_barrier(jnp.sum((doc_ends[None, :] <= positions[:, None]).astype(jnp.int32), axis=1)).astype(jnp.int32)

def reference(queries, rotated_keys, value_vectors, doc_lengths, owner_lists, out_weight):
    doc_ends = jnp.cumsum(doc_lengths).astype(jnp.int32)
    row_width = queries.shape[1]
    group_width = QUERY_HEAD_COUNT // KEY_VALUE_HEADS
    rows_per_block = 128
    reached_blocks = (MAXDOC + rows_per_block - 2) // rows_per_block + 1
    score_scale = 1.0 / math.sqrt(HEAD_SIZE)
    query_head_rows = queries.reshape(PACKED_TOKENS, KEY_VALUE_HEADS, group_width, HEAD_SIZE)
    key_head_rows = rotated_keys.reshape(PACKED_TOKENS, KEY_VALUE_HEADS, HEAD_SIZE)
    value_head_rows = value_vectors.reshape(PACKED_TOKENS, KEY_VALUE_HEADS, HEAD_SIZE)
    within = jnp.arange(rows_per_block, dtype=jnp.int32)

    def block_out(block_index):
        query_start = (block_index * rows_per_block).astype(jnp.int32)
        query_pos = query_start + within
        query_doc = doc_index(doc_ends, query_pos)
        query_block = lax.dynamic_slice_in_dim(query_head_rows, query_start, rows_per_block, 0).astype(jnp.float32)

        def tile(step_back):
            key_start = (jnp.maximum(block_index - step_back, 0) * rows_per_block).astype(jnp.int32)
            key_pos = key_start + within
            key_doc = doc_index(doc_ends, key_pos)
            key_block = lax.dynamic_slice_in_dim(key_head_rows, key_start, rows_per_block, 0).astype(jnp.float32)
            value_block = lax.dynamic_slice_in_dim(value_head_rows, key_start, rows_per_block, 0).astype(jnp.float32)
            scores = jnp.einsum('rkgd,ckd->kgrc', query_block, key_block) * score_scale
            admitted = (query_doc[:, None] == key_doc[None, :]) & (key_pos[None, :] <= query_pos[:, None])
            return (scores, admitted, value_block)

        def active(step_back):
            last_pos = (jnp.maximum(block_index - step_back, 0) * rows_per_block + rows_per_block - 1).astype(jnp.int32)
            last_doc = doc_index(doc_ends, last_pos[None])[0]
            return (block_index - step_back >= 0) & (last_doc >= query_doc[0])

        def largest_step(step_back, row_ceiling):

            def compute(carried):
                scores, admitted, unused = tile(step_back)
                return jnp.maximum(carried, lax.optimization_barrier(jnp.max(jnp.where(admitted, scores, negative_fill), axis=3)))
            return lax.cond(active(step_back), compute, lambda carried: carried, row_ceiling)
        row_ceiling = lax.fori_loop(0, reached_blocks, largest_step, jnp.full((KEY_VALUE_HEADS, group_width, rows_per_block), negative_fill, jnp.float32))

        def sum_step(step_back, sums):

            def compute(carried):
                row_total, weighted = carried
                scores, admitted, value_block = tile(step_back)
                weights = jnp.where(admitted, jnp.exp(scores - row_ceiling[..., None]), 0.0)
                rounded = lax.optimization_barrier(weights.astype(jnp.bfloat16)).astype(jnp.float32)
                return (row_total + lax.optimization_barrier(jnp.sum(weights, axis=3)), weighted + jnp.einsum('kgrc,ckd->rkgd', rounded, value_block))
            return lax.cond(active(step_back), compute, lambda carried: carried, sums)
        initial_sums = (jnp.zeros((KEY_VALUE_HEADS, group_width, rows_per_block), jnp.float32), jnp.zeros((rows_per_block, KEY_VALUE_HEADS, group_width, HEAD_SIZE), jnp.float32))
        row_total, weighted = lax.fori_loop(0, reached_blocks, sum_step, initial_sums)
        attended = weighted / jnp.transpose(row_total, (2, 0, 1))[..., None]
        return attended.astype(jnp.bfloat16).reshape(rows_per_block, row_width)
    packed = lax.map(block_out, jnp.arange(PACKED_TOKENS // rows_per_block, dtype=jnp.int32)).reshape(PACKED_TOKENS, row_width)
    owners = jnp.arange(N_CTX, dtype=jnp.int32)
    granule_of = lax.optimization_barrier(jnp.sum(jnp.where(owner_lists[None, :, :] == owners[:, None, None], owners[None, None, :], 0), axis=2))
    source = (owners[None, :] * N_CTX + granule_of).reshape(-1).astype(jnp.int32)
    owner_rows = packed.reshape(N_CTX * N_CTX, G, row_width)[source].reshape(PACKED_TOKENS, row_width)
    return jnp.dot(owner_rows, out_weight.T, preferred_element_type=jnp.float32).astype(jnp.bfloat16)
```

```python
import functools
import math

import jax
import jax.numpy as jnp
from jax import lax
from jax.experimental import pallas as pl
from jax.experimental.pallas import tpu as pltpu
from jax.sharding import Mesh
from jax.sharding import PartitionSpec as P

HEAD = 128
BLOCK = 128
NEG = -1e30
BF16 = jnp.bfloat16
F32 = jnp.float32
NZ, NY, NC = 8, 4, 2
ROW = NY * NC
CTX = NZ * ROW
CHIPS = NZ * NY
REACH = 4


def attend_kernel(place_ref, homes_ref, ends_ref, q_ref, *refs):
    mine, other, out_ref = refs[: REACH + 1], refs[REACH + 1 : 2 * REACH + 2], refs[-1]
    index, core = place_ref[0], place_ref[1]
    rows = lax.broadcasted_iota(jnp.int32, (BLOCK, BLOCK), 0)
    lanes = lax.broadcasted_iota(jnp.int32, (BLOCK, BLOCK), 1)
    chosen = (homes_ref[...] == rows % CTX) & (lanes % 2 == rows // CTX)
    query_pos = index * BLOCK + jnp.sum(jnp.where(chosen, lanes, 0), axis=1, keepdims=True)
    ends = ends_ref[...]
    doc_start = jnp.max(jnp.where(ends <= query_pos, ends, 0), axis=1, keepdims=True)
    queries = jnp.dot(
        jnp.where(chosen, 1.0, 0.0).astype(BF16), q_ref[...], preferred_element_type=F32
    ).astype(BF16)

    parts = [ref[...] for ref in mine]
    starts = [index - 2 * s for s in range(REACH + 1)]
    for s in range(REACH):
        parts.append(jnp.where(core == 0, other[s + 1][...], other[s][...]))
        starts.append(jnp.where(core == 0, index + 1 - 2 * (s + 1), index - 1 - 2 * s))
    lane_row = lax.broadcasted_iota(jnp.int32, (1, BLOCK), 1)
    key_pos = jnp.concatenate([start * BLOCK + lane_row for start in starts], axis=1)
    admitted = (key_pos <= query_pos) & (key_pos >= doc_start)
    bias = jnp.where(admitted, 0.0, NEG)

    kv_heads = parts[0].shape[1] // HEAD // 2
    heads = q_ref.shape[1] // HEAD
    group = heads // kv_heads
    scale = math.log2(math.e) / math.sqrt(HEAD)
    for k in range(kv_heads):
        keys = jnp.concatenate([p[:, k * HEAD : (k + 1) * HEAD] for p in parts], axis=0)
        first = (kv_heads + k) * HEAD
        values = jnp.concatenate([p[:, first : first + HEAD] for p in parts], axis=0)
        step = 2
        for g in range(0, group, step):
            columns = [(k * group + g + n) * HEAD for n in range(step)]
            stacked = jnp.concatenate([queries[:, c : c + HEAD] for c in columns], axis=0)
            scores = lax.dot_general(
                stacked, keys, (((1,), (1,)), ((), ())), preferred_element_type=F32
            )
            scores = scores + jnp.concatenate([bias] * step, axis=0)
            top = jnp.max(scores, axis=1, keepdims=True)
            weights = jnp.exp2((scores - top) * scale)
            total = jnp.sum(weights, axis=1, keepdims=True)
            summed = jnp.dot(weights.astype(BF16), values, preferred_element_type=F32)
            attended = (summed / total).astype(BF16)
            for n, c in enumerate(columns):
                out_ref[:, c : c + HEAD] = attended[n * BLOCK : (n + 1) * BLOCK]


def project_kernel(a_ref, w_ref, o_ref):
    product = lax.dot_general(
        a_ref[...], w_ref[...], (((1,), (1,)), ((), ())), preferred_element_type=F32
    ).astype(BF16)
    for part in range(o_ref.shape[0]):
        o_ref[part] = product[:, part * 128 : (part + 1) * 128]


def reduce_kernel(x_ref, o_ref, total):
    total[...] = functools.reduce(jnp.add, [x_ref[p].astype(F32) for p in range(x_ref.shape[0])])
    for owner in range(CTX):
        o_ref[owner] = total[pl.ds(owner, 16, stride=CTX), :].astype(BF16)


def place_kernel(x_ref, o_ref):
    for z in range(NZ):
        for y in range(NY):
            pair = [x_ref[(z * NY + y) * NC + c].astype(F32) for c in range(NC)]
            for half in range(2):
                joined = jnp.concatenate([p[:, half * 64 : half * 64 + 64] for p in pair], axis=1)
                o_ref[z * 16 : z * 16 + 16, half * 512 + y * 128 : half * 512 + y * 128 + 128] = (
                    joined.astype(BF16)
                )


def call(kernel, out_shape, flops, moved, **kwargs):
    return pl.pallas_call(
        kernel,
        out_shape=out_shape,
        cost_estimate=pl.CostEstimate(flops=flops, bytes_accessed=moved, transcendentals=0),
        compiler_params=pltpu.CompilerParams(vmem_limit_bytes=48 << 20),
        **kwargs,
    )


def chip_shift(value, steps):
    pairs = [
        (chip * NC + core, (chip + steps) * NC + core)
        for chip in range(CHIPS - steps)
        for core in range(NC)
    ]
    return lax.ppermute(value, ("z", "y", "core"), pairs)


def core_swap(value):
    return lax.ppermute(value, "core", [(0, 1), (1, 0)])


def on_device(queries, rotated_keys, value_vectors, doc_lengths, owner_lists, out_weight):
    index = lax.axis_index(("z", "y", "core")).astype(jnp.int32)
    core = lax.axis_index("core").astype(jnp.int32)
    tokens, row_width = queries.shape
    vmem = pl.BlockSpec(memory_space=pltpu.VMEM)
    smem = pl.BlockSpec(memory_space=pltpu.SMEM)

    weight = lax.all_gather(out_weight, "z", axis=0, tiled=True)

    own = jnp.concatenate([rotated_keys, value_vectors], axis=1)
    mine = [own] + [chip_shift(own, s) for s in range(1, REACH + 1)]
    other = [core_swap(v) for v in mine]

    order = jnp.arange(doc_lengths.shape[0])
    ends = jnp.sum(jnp.where(order[None, :] <= order[:, None], doc_lengths[None, :], 0), axis=1)
    ends = jnp.pad(ends, (0, BLOCK - ends.shape[0]), constant_values=1 << 30).reshape(1, BLOCK)
    homes = lax.dynamic_slice_in_dim(owner_lists, index, 1, axis=0)
    homes = jnp.broadcast_to(homes[:, :, None], (1, CTX, tokens // CTX)).reshape(1, tokens)
    place = jnp.stack([index, core])

    attended = call(
        attend_kernel,
        jax.ShapeDtypeStruct(queries.shape, BF16),
        4 * tokens * row_width * 9 * BLOCK,
        10 << 20,
        in_specs=[smem] + [vmem] * (3 + 2 * (REACH + 1)),
        out_specs=vmem,
    )(place, homes.astype(jnp.int32), ends.astype(jnp.int32), queries, *mine, *other)

    rows = lax.all_gather(attended, ("y", "core"), axis=0, tiled=True)
    step = 256
    features = weight.shape[0]
    shares = call(
        project_kernel,
        jax.ShapeDtypeStruct((features // 128, rows.shape[0], 128), BF16),
        2 * rows.shape[0] * features * row_width,
        7 << 20,
        grid=(rows.shape[0] // step,),
        in_specs=[
            pl.BlockSpec((step, row_width), lambda m: (m, 0)),
            pl.BlockSpec((features, row_width), lambda m: (0, 0)),
        ],
        out_specs=pl.BlockSpec((features // 128, step, 128), lambda m: (0, m, 0)),
    )(rows, weight)

    shares = lax.all_to_all(shares, "tp", 0, 0, tiled=True)
    sent = call(
        reduce_kernel,
        jax.ShapeDtypeStruct((CTX, 16, 128), BF16),
        4 << 20,
        2 << 20,
        in_specs=[vmem],
        out_specs=vmem,
        scratch_shapes=[pltpu.VMEM((rows.shape[0], 128), F32)],
    )(shares)
    received = lax.all_to_all(sent, ("z", "y", "core"), 0, 0, tiled=True)
    return call(
        place_kernel,
        jax.ShapeDtypeStruct((tokens, features * 2), BF16),
        1 << 20,
        1 << 19,
        in_specs=[vmem],
        out_specs=vmem,
    )(received)


def solution(mesh):
    split = Mesh(mesh.devices.reshape(NZ, NY, NC, -1), ("z", "y", "core", "tp"))
    ctx = ("z", "y", "core")
    placed = (P(ctx, "tp"), P(ctx, "tp"), P(ctx, "tp"), P(), P(), P(ctx, "tp"))
    return jax.shard_map(
        on_device, mesh=split, in_specs=placed, out_specs=P(ctx, "tp"), check_vma=False
    )
```

```python
import functools
import math

import jax
import jax.numpy as jnp
from jax import lax
from jax.experimental import pallas as pl
from jax.experimental.pallas import tpu as pltpu
from jax.sharding import Mesh
from jax.sharding import PartitionSpec as P

HEAD = 128
BLOCK = 128
NEG = -1e30
BF16 = jnp.bfloat16
F32 = jnp.float32
NZ, NY, NC = 8, 4, 2
ROW = NY * NC
CTX = NZ * ROW
CHIPS = NZ * NY
REACH = 4


def attend_kernel(place_ref, homes_ref, ends_ref, q_ref, *refs):
    mine, other, out_ref = refs[: REACH + 1], refs[REACH + 1 : 2 * REACH + 2], refs[-1]
    index, core = place_ref[0], place_ref[1]
    rows = lax.broadcasted_iota(jnp.int32, (BLOCK, BLOCK), 0)
    lanes = lax.broadcasted_iota(jnp.int32, (BLOCK, BLOCK), 1)
    chosen = (homes_ref[...] == rows % CTX) & (lanes % 2 == rows // CTX)
    query_pos = index * BLOCK + jnp.sum(jnp.where(chosen, lanes, 0), axis=1, keepdims=True)
    ends = ends_ref[...]
    doc_start = jnp.max(jnp.where(ends <= query_pos, ends, 0), axis=1, keepdims=True)
    queries = jnp.dot(
        jnp.where(chosen, 1.0, 0.0).astype(BF16), q_ref[...], preferred_element_type=F32
    ).astype(BF16)

    parts = [ref[...] for ref in mine]
    starts = [index - 2 * s for s in range(REACH + 1)]
    for s in range(REACH):
        parts.append(jnp.where(core == 0, other[s + 1][...], other[s][...]))
        starts.append(jnp.where(core == 0, index + 1 - 2 * (s + 1), index - 1 - 2 * s))
    lane_row = lax.broadcasted_iota(jnp.int32, (1, BLOCK), 1)
    key_pos = jnp.concatenate([start * BLOCK + lane_row for start in starts], axis=1)
    admitted = (key_pos <= query_pos) & (key_pos >= doc_start)
    bias = jnp.where(admitted, 0.0, NEG)

    kv_heads = parts[0].shape[1] // HEAD // 2
    heads = q_ref.shape[1] // HEAD
    group = heads // kv_heads
    scale = math.log2(math.e) / math.sqrt(HEAD)
    for k in range(kv_heads):
        keys = jnp.concatenate([p[:, k * HEAD : (k + 1) * HEAD] for p in parts], axis=0)
        first = (kv_heads + k) * HEAD
        values = jnp.concatenate([p[:, first : first + HEAD] for p in parts], axis=0)
        step = 2
        for g in range(0, group, step):
            columns = [(k * group + g + n) * HEAD for n in range(step)]
            stacked = jnp.concatenate([queries[:, c : c + HEAD] for c in columns], axis=0)
            scores = lax.dot_general(
                stacked, keys, (((1,), (1,)), ((), ())), preferred_element_type=F32
            )
            scores = scores + jnp.concatenate([bias] * step, axis=0)
            top = jnp.max(scores, axis=1, keepdims=True)
            weights = jnp.exp2((scores - top) * scale)
            total = jnp.sum(weights, axis=1, keepdims=True)
            summed = jnp.dot(weights.astype(BF16), values, preferred_element_type=F32)
            attended = (summed / total).astype(BF16)
            for n, c in enumerate(columns):
                out_ref[:, c : c + HEAD] = attended[n * BLOCK : (n + 1) * BLOCK]


def join_kernel(k_ref, v_ref, o_ref):
    width = k_ref.shape[1]
    o_ref[:, :width] = k_ref[...]
    o_ref[:, width:] = v_ref[...]


def project_kernel(turn_ref, w_ref, *refs):
    blocks, outs = refs[:-4], refs[-4:]
    rows = jnp.concatenate([ref[...] for ref in blocks], axis=0)
    for pair in range(2):
        weight = jnp.concatenate(
            [
                w_ref[pl.ds(pl.multiple_of(((turn_ref[0] + d) % 4) * 128, 128), 128), :]
                for d in (2 * pair, 2 * pair + 1)
            ],
            axis=0,
        )
        product = lax.dot_general(
            rows, weight, (((1,), (1,)), ((), ())), preferred_element_type=F32
        )
        for n in range(2):
            out = outs[2 * pair + n]
            out[...] = product[:, n * 128 : (n + 1) * 128].astype(out.dtype)


def reduce_kernel(place_ref, *refs):
    shares, o_ref, total = refs[:-2], refs[-2], refs[-1]
    y, core = place_ref[0], place_ref[1]
    sources = [(0, 0), (0, 1), (3, 0), (3, 1), (1, 0), (1, 1), (2, 0), (2, 1)]
    block = 0
    for chunk in range(3):
        own = shares[4 * chunk]
        summed = own[...]
        for n in range(1, 4):
            summed = summed + shares[4 * chunk + n][...].astype(F32)
        for first in range(0, own.shape[0], BLOCK):
            dy, dc = sources[block]
            row = (((y + dy) % NY) * NC + (core + dc) % NC) * BLOCK
            total[pl.ds(pl.multiple_of(row, BLOCK), BLOCK), :] = summed[first : first + BLOCK]
            block += 1
    for owner in range(CTX):
        o_ref[owner] = total[pl.ds(owner, 16, stride=CTX), :].astype(BF16)


def place_kernel(x_ref, o_ref):
    for z in range(NZ):
        for y in range(NY):
            pair = [x_ref[(z * NY + y) * NC + c].astype(F32) for c in range(NC)]
            for half in range(2):
                joined = jnp.concatenate([p[:, half * 64 : half * 64 + 64] for p in pair], axis=1)
                o_ref[z * 16 : z * 16 + 16, half * 512 + y * 128 : half * 512 + y * 128 + 128] = (
                    joined.astype(BF16)
                )


def call(kernel, out_shape, flops, moved, **kwargs):
    return pl.pallas_call(
        kernel,
        out_shape=out_shape,
        cost_estimate=pl.CostEstimate(flops=flops, bytes_accessed=moved, transcendentals=0),
        compiler_params=pltpu.CompilerParams(vmem_limit_bytes=48 << 20),
        **kwargs,
    )


def chip_shift(value, steps):
    pairs = [
        (chip * NC + core, (chip + steps) % CHIPS * NC + core)
        for chip in range(CHIPS)
        for core in range(NC)
    ]
    return lax.ppermute(value, ("z", "y", "core"), pairs)


def ring_shift(value, axis, steps):
    count = lax.axis_size(axis)
    return lax.ppermute(value, axis, [(n, (n + steps) % count) for n in range(count)])


def core_swap(value):
    return lax.ppermute(value, "core", [(0, 1), (1, 0)])


def on_device(queries, rotated_keys, value_vectors, doc_lengths, owner_lists, out_weight):
    index = lax.axis_index(("z", "y", "core")).astype(jnp.int32)
    core = lax.axis_index("core").astype(jnp.int32)
    tokens, row_width = queries.shape
    vmem = pl.BlockSpec(memory_space=pltpu.VMEM)
    smem = pl.BlockSpec(memory_space=pltpu.SMEM)

    weight = lax.all_gather(out_weight, "z", axis=0, tiled=True)

    own = call(
        join_kernel,
        jax.ShapeDtypeStruct((tokens, 2 * rotated_keys.shape[1]), BF16),
        0,
        1 << 18,
        in_specs=[vmem, vmem],
        out_specs=vmem,
    )(rotated_keys, value_vectors)
    mine = [own] + [chip_shift(own, s) for s in range(1, REACH + 1)]
    other = [core_swap(v) for v in mine]

    order = jnp.arange(doc_lengths.shape[0])
    ends = jnp.sum(jnp.where(order[None, :] <= order[:, None], doc_lengths[None, :], 0), axis=1)
    ends = jnp.pad(ends, (0, BLOCK - ends.shape[0]), constant_values=1 << 30).reshape(1, BLOCK)
    homes = lax.dynamic_slice_in_dim(owner_lists, index, 1, axis=0)
    homes = jnp.broadcast_to(homes[:, :, None], (1, CTX, tokens // CTX)).reshape(1, tokens)
    place = jnp.stack([index, core])

    attended = call(
        attend_kernel,
        jax.ShapeDtypeStruct(queries.shape, BF16),
        4 * tokens * row_width * 9 * BLOCK,
        10 << 20,
        in_specs=[smem] + [vmem] * (3 + 2 * (REACH + 1)),
        out_specs=vmem,
    )(place, homes.astype(jnp.int32), ends.astype(jnp.int32), queries, *mine, *other)

    turn = lax.axis_index("tp").astype(jnp.int32).reshape(1)
    features = weight.shape[0]

    def project(blocks):
        rows = sum(block.shape[0] for block in blocks)
        shape = (rows, 128)
        shares = call(
            project_kernel,
            [jax.ShapeDtypeStruct(shape, F32)] + [jax.ShapeDtypeStruct(shape, BF16)] * 3,
            2 * rows * features * row_width,
            (2 << 20) + rows * (2 * row_width + 1280),
            in_specs=[smem] + [vmem] * (1 + len(blocks)),
            out_specs=[vmem] * 4,
        )(turn, weight, *blocks)
        return [shares[0]] + [ring_shift(shares[d], "tp", d) for d in (1, 3, 2)]

    half = tokens // 2
    below, above = ring_shift(attended, "y", 1), ring_shift(attended, "y", -1)
    shares = project([attended, core_swap(attended)])
    far = [ring_shift(below[:half], "y", 1), ring_shift(above[half:], "y", -1)]
    shares += project([below, core_swap(below), above, core_swap(above)])
    shares += project(far + [core_swap(v) for v in far])

    sent = call(
        reduce_kernel,
        jax.ShapeDtypeStruct((CTX, 16, 128), BF16),
        4 << 20,
        2 << 20,
        in_specs=[smem] + [vmem] * 12,
        out_specs=vmem,
        scratch_shapes=[pltpu.VMEM((ROW * tokens, 128), F32)],
    )(jnp.stack([lax.axis_index("y").astype(jnp.int32), core]), *shares)
    received = lax.all_to_all(sent, ("z", "y", "core"), 0, 0, tiled=True)
    return call(
        place_kernel,
        jax.ShapeDtypeStruct((tokens, features * 2), BF16),
        1 << 20,
        1 << 19,
        in_specs=[vmem],
        out_specs=vmem,
    )(received)


def solution(mesh):
    split = Mesh(mesh.devices.reshape(NZ, NY, NC, -1), ("z", "y", "core", "tp"))
    ctx = ("z", "y", "core")
    placed = (P(ctx, "tp"), P(ctx, "tp"), P(ctx, "tp"), P(), P(), P(ctx, "tp"))
    return jax.shard_map(
        on_device, mesh=split, in_specs=placed, out_specs=P(ctx, "tp"), check_vma=False
    )
```

```python
import functools
import math

import jax
import jax.numpy as jnp
from jax import lax
from jax.experimental import pallas as pl
from jax.experimental.pallas import tpu as pltpu
from jax.sharding import Mesh
from jax.sharding import PartitionSpec as P

HEAD = 128
BLOCK = 128
NEG = -1e30
BF16 = jnp.bfloat16
F32 = jnp.float32
NZ, NY, NC, NX = 8, 4, 2, 4
ROW = NY * NC
CTX = NZ * ROW
CHIPS = NZ * NY
REACH = 4
KEYS = 2 * (REACH + 1) * BLOCK
CHUNKS = [(0, 1, NY - 1), (2,)]


def fetch(copies):
    for copy in copies:
        copy.start()
    for copy in copies:
        copy.wait()


def join_kernel(k_ref, v_ref, o_ref, sems):
    width = k_ref.shape[1]
    fetch(
        [
            pltpu.make_async_copy(ref, o_ref.at[:, n * width : (n + 1) * width], sems.at[n])
            for n, ref in enumerate((k_ref, v_ref))
        ]
    )


def prepare_kernel(place_ref, homes_ref, ends_ref, q_ref, keep_ref, give_ref, bias_ref):
    index, core = place_ref[0], place_ref[1]
    swapped = index + 1 - 2 * core
    rows = lax.broadcasted_iota(jnp.int32, (BLOCK, BLOCK), 0)
    lanes = lax.broadcasted_iota(jnp.int32, (BLOCK, BLOCK), 1)
    parity = lanes % 2 == rows // CHIPS % 2
    half = rows // CTX
    own, other = homes_ref[0:1, :], homes_ref[1:2, :]

    select = (own == rows % CHIPS * NC + (half + core) % NC) & parity
    queries = jnp.dot(
        jnp.where(select, 1.0, 0.0).astype(BF16), q_ref[...], preferred_element_type=F32
    ).astype(BF16)
    keep_ref[...] = queries[:CTX]
    give_ref[...] = queries[CTX:]

    attended = (jnp.where(half == 0, own, other) == rows % CHIPS * NC + core) & parity
    token = jnp.sum(jnp.where(attended, lanes, 0), axis=1, keepdims=True)
    query_pos = jnp.where(half[:, :1] == 0, index, swapped) * BLOCK + token
    ends = ends_ref[...]
    doc_start = jnp.max(jnp.where(ends <= query_pos, ends, 0), axis=1, keepdims=True)
    blocks = [start - 2 * s for start in (index, swapped) for s in range(REACH + 1)]
    for n, block in enumerate(blocks):
        key_pos = block * BLOCK + lanes
        admitted = (key_pos <= query_pos) & (key_pos >= doc_start)
        bias_ref[:, n * BLOCK : (n + 1) * BLOCK] = jnp.where(admitted, 0.0, NEG)


def attend_kernel(bias_ref, keep_ref, got_ref, *refs):
    blocks, out_ref = refs[:-1], refs[-1]
    kv_heads = blocks[0].shape[1] // HEAD // 2
    group = keep_ref.shape[1] // HEAD // kv_heads

    scale = math.log2(math.e) / math.sqrt(HEAD)
    step = 2
    bias = jnp.concatenate([bias_ref[...]] * step, axis=0)
    for k in range(kv_heads):
        keys, values = [
            jnp.concatenate([ref[:, n * HEAD : (n + 1) * HEAD] for ref in blocks], axis=0)
            for n in (k, kv_heads + k)
        ]
        for g in range(0, group, step):
            columns = [(k * group + g + n) * HEAD for n in range(step)]
            stacked = jnp.concatenate(
                [ref[:, c : c + HEAD] for c in columns for ref in (keep_ref, got_ref)], axis=0
            )
            scores = lax.dot_general(
                stacked, keys, (((1,), (1,)), ((), ())), preferred_element_type=F32
            )
            scores = scores + bias
            top = jnp.max(scores, axis=1, keepdims=True)
            weights = jnp.exp2((scores - top) * scale)
            total = jnp.sum(weights, axis=1, keepdims=True)
            summed = jnp.dot(weights.astype(BF16), values, preferred_element_type=F32)
            attended = (summed / total).astype(BF16)
            for n, c in enumerate(columns):
                out_ref[:, c : c + HEAD] = attended[n * BLOCK : (n + 1) * BLOCK]


def project_kernel(x_ref, w_ref, *refs):
    *refs, sorted_ref, sems = refs
    blocks, outs = refs[:-NX], refs[-NX:]
    width = w_ref.shape[0] // NX
    copies = [
        pltpu.make_async_copy(
            w_ref.at[pl.ds(pl.multiple_of((x_ref[0] + n) % NX * width, width), width), :],
            sorted_ref.at[n],
            sems.at[n],
        )
        for n in range(NX)
    ]
    for copy in copies:
        copy.start()
    rows = jnp.concatenate([ref[...] for ref in blocks], axis=0)
    for n, out in enumerate(outs):
        copies[n].wait()
        out[...] = lax.dot_general(
            rows, sorted_ref[n], (((1,), (1,)), ((), ())), preferred_element_type=F32
        ).astype(out.dtype)


def reduce_kernel(place_ref, *refs):
    shares, o_ref, total = refs[:-2], refs[-2], refs[-1]
    y, core = place_ref[0], place_ref[1]
    for chunk, sources in enumerate(CHUNKS):
        summed = shares[NX * chunk][...]
        for n in range(1, NX):
            summed = summed + shares[NX * chunk + n][...].astype(F32)
        for n in range(len(sources) * NC):
            row = ((y + sources[n // NC]) % NY * NC + (core + n) % NC) * CTX
            for half in range(2):
                total[half, pl.ds(pl.multiple_of(row, CTX), CTX), :] = summed[
                    n * CTX : (n + 1) * CTX, half * 128 : half * 128 + 128
                ]
    for half in range(2):
        for chip in range(CHIPS):
            o_ref[chip, :, half * 128 : half * 128 + 128] = total[
                half, pl.ds(chip, 16, stride=CHIPS), :
            ].astype(BF16)


def place_kernel(x_ref, o_ref):
    for z in range(NZ):
        for y in range(NY):
            for half in range(2):
                column = half * 512 + y * 128
                o_ref[z * 16 : z * 16 + 16, column : column + 128] = x_ref[
                    z * NY + y, :, half * 128 : half * 128 + 128
                ]


def call(kernel, out_shape, flops, moved, vmem=16, **kwargs):
    return pl.pallas_call(
        kernel,
        out_shape=out_shape,
        cost_estimate=pl.CostEstimate(flops=flops, bytes_accessed=moved, transcendentals=0),
        compiler_params=pltpu.CompilerParams(vmem_limit_bytes=vmem << 20),
        **kwargs,
    )


def chip_shift(value, steps):
    pairs = [
        (chip * NC + core, (chip + steps) % CHIPS * NC + core)
        for chip in range(CHIPS)
        for core in range(NC)
    ]
    return lax.ppermute(value, ("z", "y", "core"), pairs)


def ring_shift(value, axis, steps):
    count = lax.axis_size(axis)
    return lax.ppermute(value, axis, [(n, (n + steps) % count) for n in range(count)])


def core_swap(value):
    return lax.ppermute(value, "core", [(0, 1), (1, 0)])


def after(value, *earlier):
    return lax.optimization_barrier((value, *earlier))[0]


def on_device(queries, rotated_keys, value_vectors, doc_lengths, owner_lists, out_weight):
    index = lax.axis_index(("z", "y", "core")).astype(jnp.int32)
    at = {name: lax.axis_index(name).astype(jnp.int32) for name in ("z", "y", "core", "tp")}
    tokens, row_width = queries.shape
    vmem = pl.BlockSpec(memory_space=pltpu.VMEM)
    smem = pl.BlockSpec(memory_space=pltpu.SMEM)
    hbm = pl.BlockSpec(memory_space=pltpu.HBM)

    weight = lax.all_gather(out_weight, ("z", "core"), axis=0, tiled=True)
    features = weight.shape[0]

    own = call(
        join_kernel,
        jax.ShapeDtypeStruct((tokens, 2 * rotated_keys.shape[1]), BF16),
        0,
        1 << 18,
        in_specs=[hbm] * 2,
        out_specs=vmem,
        scratch_shapes=[pltpu.SemaphoreType.DMA((2,))],
    )(rotated_keys, value_vectors)
    mine = [own] + [chip_shift(own, s) for s in range(1, REACH + 1)]
    other = [core_swap(v) for v in mine]

    order = jnp.arange(doc_lengths.shape[0])
    ends = jnp.sum(jnp.where(order[None, :] <= order[:, None], doc_lengths[None, :], 0), axis=1)
    ends = jnp.pad(ends, (0, BLOCK - ends.shape[0]), constant_values=1 << 30).reshape(1, BLOCK)
    pair = lax.dynamic_slice_in_dim(owner_lists, index - at["core"], NC, axis=0)
    pair = jnp.where(at["core"] == 0, pair, pair[::-1])
    homes = jnp.broadcast_to(pair[:, :, None], (NC, CTX, tokens // CTX)).reshape(NC, tokens)
    half_rows = jax.ShapeDtypeStruct((tokens // 2, row_width), BF16)
    keep, give, bias = call(
        prepare_kernel,
        [half_rows, half_rows, jax.ShapeDtypeStruct((tokens, KEYS), F32)],
        2 * tokens * tokens * row_width,
        2 << 20,
        in_specs=[smem] + [vmem] * 3,
        out_specs=[vmem] * 3,
    )(
        jnp.stack([index, at["core"]]),
        homes.astype(jnp.int32),
        ends.astype(jnp.int32),
        queries,
    )
    attended = call(
        attend_kernel,
        jax.ShapeDtypeStruct((tokens, row_width), BF16),
        4 * tokens * row_width * KEYS,
        8 << 20,
        in_specs=[vmem] * (3 + 2 * (REACH + 1)),
        out_specs=vmem,
    )(bias, keep, core_swap(give), *mine, *other)
    rows = {0: attended} | {d: ring_shift(attended, "y", -d) for d in (1, 3)}
    rows[2] = ring_shift(after(attended, rows[1], rows[3]), "y", 2)

    def project(blocks):
        count = sum(block.shape[0] for block in blocks)
        shape = (count, features // NX)
        shares = call(
            project_kernel,
            [jax.ShapeDtypeStruct(shape, F32)] + [jax.ShapeDtypeStruct(shape, BF16)] * 3,
            2 * count * features * row_width,
            (4 << 20) + count * (2 * row_width + 2560),
            in_specs=[smem, hbm] + [vmem] * len(blocks),
            out_specs=[vmem] * NX,
            scratch_shapes=[
                pltpu.VMEM((NX, features // NX, row_width), BF16),
                pltpu.SemaphoreType.DMA((NX,)),
            ],
        )(at["tp"].reshape(1), weight, *blocks)
        return [shares[0]] + [ring_shift(shares[d], "tp", d) for d in (1, 3, 2)]

    shares = []
    for chunk in CHUNKS:
        shares += project([rows[d] for d in chunk])
    sent = call(
        reduce_kernel,
        jax.ShapeDtypeStruct((CHIPS, 16, features // NX), BF16),
        4 << 20,
        2 << 20,
        in_specs=[smem] + [vmem] * len(shares),
        out_specs=vmem,
        scratch_shapes=[pltpu.VMEM((2, ROW * CTX, 128), F32)],
    )(jnp.stack([at["y"], at["core"]]), *shares)
    received = lax.all_to_all(sent, ("z", "y"), 0, 0, tiled=True)
    return call(
        place_kernel,
        jax.ShapeDtypeStruct((tokens, features), BF16),
        1 << 20,
        1 << 19,
        in_specs=[vmem],
        out_specs=vmem,
    )(received)


def solution(mesh):
    split = Mesh(mesh.devices.reshape(NZ, NY, NC, NX), ("z", "y", "core", "tp"))
    ctx = ("z", "y", "core")
    placed = (P(ctx, "tp"), P(ctx, "tp"), P(ctx, "tp"), P(), P(), P(ctx, "tp"))
    return jax.shard_map(
        on_device, mesh=split, in_specs=placed, out_specs=P(ctx, "tp"), check_vma=False
    )
```

```python
import functools
import math

import jax
import jax.numpy as jnp
from jax import lax
from jax.experimental import pallas as pl
from jax.experimental.pallas import tpu as pltpu
from jax.sharding import Mesh
from jax.sharding import PartitionSpec as P

HEAD = 128
BLOCK = 128
NEG = -1e30
BF16 = jnp.bfloat16
F32 = jnp.float32
NZ, NY, NC, NX = 8, 4, 2, 4
ROW = NY * NC
CTX = NZ * ROW
CHIPS = NZ * NY
REACH = 4
KEYS = 2 * (REACH + 1) * BLOCK
PROJECT_VMEM = 52
OFFSETS = [0, -1, 1, -2, 2, -3, 3, 4, 4]
CHUNKS = [(0, 1, NY - 1), (2,)]


def fetch(copies):
    for copy in copies:
        copy.start()
    for copy in copies:
        copy.wait()


def join_kernel(k_ref, v_ref, o_ref, sems):
    width = k_ref.shape[1]
    fetch(
        [
            pltpu.make_async_copy(ref, o_ref.at[:, n * width : (n + 1) * width], sems.at[n])
            for n, ref in enumerate((k_ref, v_ref))
        ]
    )


def prepare_kernel(place_ref, homes_ref, ends_ref, q_ref, keep_ref, give_ref, bias_ref):
    index, core = place_ref[0], place_ref[1]
    swapped = index + 1 - 2 * core
    rows = lax.broadcasted_iota(jnp.int32, (BLOCK, BLOCK), 0)
    lanes = lax.broadcasted_iota(jnp.int32, (BLOCK, BLOCK), 1)
    parity = lanes % 2 == rows // CHIPS % 2
    half = rows // CTX
    own, other = homes_ref[0:1, :], homes_ref[1:2, :]

    select = (own == rows % CHIPS * NC + (half + core) % NC) & parity
    queries = jnp.dot(
        jnp.where(select, 1.0, 0.0).astype(BF16), q_ref[...], preferred_element_type=F32
    ).astype(BF16)
    keep_ref[...] = queries[:CTX]
    give_ref[...] = queries[CTX:]

    attended = (jnp.where(half == 0, own, other) == rows % CHIPS * NC + core) & parity
    token = jnp.sum(jnp.where(attended, lanes, 0), axis=1, keepdims=True)
    query_pos = jnp.where(half[:, :1] == 0, index, swapped) * BLOCK + token
    ends = ends_ref[...]
    doc_start = jnp.max(jnp.where(ends <= query_pos, ends, 0), axis=1, keepdims=True)
    blocks = [start - 2 * s for start in (index, swapped) for s in range(REACH + 1)]
    for n, block in enumerate(blocks):
        key_pos = block * BLOCK + lanes
        admitted = (key_pos <= query_pos) & (key_pos >= doc_start)
        bias_ref[:, n * BLOCK : (n + 1) * BLOCK] = jnp.where(admitted, 0.0, NEG)


def attend_kernel(bias_ref, keep_ref, got_ref, *refs):
    blocks, out_ref = refs[:-1], refs[-1]
    kv_heads = blocks[0].shape[1] // HEAD // 2
    group = keep_ref.shape[1] // HEAD // kv_heads

    scale = math.log2(math.e) / math.sqrt(HEAD)
    step = 2
    bias = jnp.concatenate([bias_ref[...]] * step, axis=0)
    for k in range(kv_heads):
        keys, values = [
            jnp.concatenate([ref[:, n * HEAD : (n + 1) * HEAD] for ref in blocks], axis=0)
            for n in (k, kv_heads + k)
        ]
        for g in range(0, group, step):
            columns = [(k * group + g + n) * HEAD for n in range(step)]
            stacked = jnp.concatenate(
                [ref[:, c : c + HEAD] for c in columns for ref in (keep_ref, got_ref)], axis=0
            )
            scores = lax.dot_general(
                stacked, keys, (((1,), (1,)), ((), ())), preferred_element_type=F32
            )
            scores = scores + bias
            top = jnp.max(scores, axis=1, keepdims=True)
            weights = jnp.exp2((scores - top) * scale)
            total = jnp.sum(weights, axis=1, keepdims=True)
            summed = jnp.dot(weights.astype(BF16), values, preferred_element_type=F32)
            attended = (summed / total).astype(BF16)
            for n, c in enumerate(columns):
                out_ref[:, c : c + HEAD] = attended[n * BLOCK : (n + 1) * BLOCK]


def project_kernel(place_ref, *refs):
    *refs, sorted_ref, sems = refs
    count = NC * len(OFFSETS)
    pieces, blocks, outs = refs[:count], refs[count:-NX], refs[-NX:]
    z, x, core = place_ref[0], place_ref[1], place_ref[2]
    rows = pieces[0].shape[0]
    copies = []
    for side in range(NC):
        done = 0
        for n, offset in enumerate(OFFSETS):
            piece = pieces[side * len(OFFSETS) + n]
            source = (z + offset + NZ) % NZ
            row = source % 2 * 128 + (core + side) % NC * rows
            if piece.shape[0] != rows:
                row, done = row + done, done + piece.shape[0]
            target = sorted_ref.at[
                (source // 2 - x + NX) % NX, pl.ds(pl.multiple_of(row, 32), piece.shape[0]), :
            ]
            copies.append(pltpu.make_async_copy(piece, target, sems.at[len(copies)]))
    fetch(copies)
    attended = jnp.concatenate([ref[...] for ref in blocks], axis=0)
    for n, out in enumerate(outs):
        out[...] = lax.dot_general(
            attended, sorted_ref[n], (((1,), (1,)), ((), ())), preferred_element_type=F32
        ).astype(out.dtype)


def reduce_kernel(place_ref, *refs):
    shares, o_ref, total = refs[:-2], refs[-2], refs[-1]
    y, core = place_ref[0], place_ref[1]
    for chunk, sources in enumerate(CHUNKS):
        summed = shares[NX * chunk][...]
        for n in range(1, NX):
            summed = summed + shares[NX * chunk + n][...].astype(F32)
        for n in range(len(sources) * NC):
            row = ((y + sources[n // NC]) % NY * NC + (core + n) % NC) * CTX
            for half in range(2):
                total[half, pl.ds(pl.multiple_of(row, CTX), CTX), :] = summed[
                    n * CTX : (n + 1) * CTX, half * 128 : half * 128 + 128
                ]
    for half in range(2):
        for chip in range(CHIPS):
            o_ref[chip, :, half * 128 : half * 128 + 128] = total[
                half, pl.ds(chip, 16, stride=CHIPS), :
            ].astype(BF16)


def place_kernel(x_ref, o_ref):
    for z in range(NZ):
        for y in range(NY):
            for half in range(2):
                column = half * 512 + y * 128
                o_ref[z * 16 : z * 16 + 16, column : column + 128] = x_ref[
                    z * NY + y, :, half * 128 : half * 128 + 128
                ]


def call(kernel, out_shape, flops, moved, vmem=16, **kwargs):
    return pl.pallas_call(
        kernel,
        out_shape=out_shape,
        cost_estimate=pl.CostEstimate(flops=flops, bytes_accessed=moved, transcendentals=0),
        compiler_params=pltpu.CompilerParams(vmem_limit_bytes=vmem << 20),
        **kwargs,
    )


def chip_shift(value, steps):
    pairs = [
        (chip * NC + core, (chip + steps) % CHIPS * NC + core)
        for chip in range(CHIPS)
        for core in range(NC)
    ]
    return lax.ppermute(value, ("z", "y", "core"), pairs)


def ring_shift(value, axis, steps):
    count = lax.axis_size(axis)
    return lax.ppermute(value, axis, [(n, (n + steps) % count) for n in range(count)])


def core_swap(value):
    return lax.ppermute(value, "core", [(0, 1), (1, 0)])


def after(value, *earlier):
    return lax.optimization_barrier((value, *earlier))[0]


def on_device(queries, rotated_keys, value_vectors, doc_lengths, owner_lists, out_weight):
    index = lax.axis_index(("z", "y", "core")).astype(jnp.int32)
    at = {name: lax.axis_index(name).astype(jnp.int32) for name in ("z", "y", "core", "tp")}
    tokens, row_width = queries.shape
    vmem = pl.BlockSpec(memory_space=pltpu.VMEM)
    smem = pl.BlockSpec(memory_space=pltpu.SMEM)
    hbm = pl.BlockSpec(memory_space=pltpu.HBM)

    up, down = [out_weight], [out_weight]
    for _ in range(2):
        up.append(ring_shift(up[-1], "z", 1))
        down.append(ring_shift(down[-1], "z", -1))

    own = call(
        join_kernel,
        jax.ShapeDtypeStruct((tokens, 2 * rotated_keys.shape[1]), BF16),
        0,
        1 << 18,
        in_specs=[hbm] * 2,
        out_specs=vmem,
        scratch_shapes=[pltpu.SemaphoreType.DMA((2,))],
    )(rotated_keys, value_vectors)
    mine = [own] + [chip_shift(own, s) for s in range(1, REACH + 1)]
    other = [core_swap(v) for v in mine]

    order = jnp.arange(doc_lengths.shape[0])
    ends = jnp.sum(jnp.where(order[None, :] <= order[:, None], doc_lengths[None, :], 0), axis=1)
    ends = jnp.pad(ends, (0, BLOCK - ends.shape[0]), constant_values=1 << 30).reshape(1, BLOCK)
    pair = lax.dynamic_slice_in_dim(owner_lists, index - at["core"], NC, axis=0)
    pair = jnp.where(at["core"] == 0, pair, pair[::-1])
    homes = jnp.broadcast_to(pair[:, :, None], (NC, CTX, tokens // CTX)).reshape(NC, tokens)
    half_rows = jax.ShapeDtypeStruct((tokens // 2, row_width), BF16)
    keep, give, bias = call(
        prepare_kernel,
        [half_rows, half_rows, jax.ShapeDtypeStruct((tokens, KEYS), F32)],
        2 * tokens * tokens * row_width,
        2 << 20,
        in_specs=[smem] + [vmem] * 3,
        out_specs=[vmem] * 3,
    )(
        jnp.stack([index, at["core"]]),
        homes.astype(jnp.int32),
        ends.astype(jnp.int32),
        after(queries, up[1], down[1]),
    )
    attended = call(
        attend_kernel,
        jax.ShapeDtypeStruct((tokens, row_width), BF16),
        4 * tokens * row_width * KEYS,
        8 << 20,
        in_specs=[vmem] * (3 + 2 * (REACH + 1)),
        out_specs=vmem,
    )(after(bias, up[2], down[2]), keep, core_swap(give), *mine, *other)
    rows = {0: attended} | {d: ring_shift(attended, "y", -d) for d in (1, 3)}
    up.append(ring_shift(up[2], "z", 1))
    down.append(ring_shift(down[2], "z", -1))
    rows[2] = ring_shift(after(attended, rows[1], rows[3], up[3], down[3]), "y", 2)
    middle = out_weight.shape[0] // 2
    pieces = [out_weight]
    for n in range(1, 4):
        pieces += [up[n], down[n]]
    pieces += [ring_shift(up[3][:middle], "z", 1), ring_shift(down[3][middle:], "z", -1)]
    pieces += [core_swap(piece) for piece in pieces]
    features = NZ * NC * out_weight.shape[0]
    corner = jnp.stack([at["z"], at["tp"], at["core"]])

    def project(blocks):
        count = sum(block.shape[0] for block in blocks)
        shape = (count, features // NX)
        shares = call(
            project_kernel,
            [jax.ShapeDtypeStruct(shape, F32)] + [jax.ShapeDtypeStruct(shape, BF16)] * 3,
            2 * count * features * row_width,
            (4 << 20) + count * (2 * row_width + 2560),
            vmem=PROJECT_VMEM,
            in_specs=[smem] + [hbm] * len(pieces) + [vmem] * len(blocks),
            out_specs=[vmem] * NX,
            scratch_shapes=[
                pltpu.VMEM((NX, features // NX, row_width), BF16),
                pltpu.SemaphoreType.DMA((len(pieces),)),
            ],
        )(corner, *pieces, *blocks)
        return [shares[0]] + [ring_shift(shares[d], "tp", d) for d in (1, 3, 2)]

    shares = []
    for chunk in CHUNKS:
        shares += project([rows[d] for d in chunk])
    sent = call(
        reduce_kernel,
        jax.ShapeDtypeStruct((CHIPS, 16, features // NX), BF16),
        4 << 20,
        2 << 20,
        in_specs=[smem] + [vmem] * len(shares),
        out_specs=vmem,
        scratch_shapes=[pltpu.VMEM((2, ROW * CTX, 128), F32)],
    )(jnp.stack([at["y"], at["core"]]), *shares)
    received = lax.all_to_all(sent, ("z", "y"), 0, 0, tiled=True)
    return call(
        place_kernel,
        jax.ShapeDtypeStruct((tokens, features), BF16),
        1 << 20,
        1 << 19,
        in_specs=[vmem],
        out_specs=vmem,
    )(received)


def solution(mesh):
    split = Mesh(mesh.devices.reshape(NZ, NY, NC, NX), ("z", "y", "core", "tp"))
    ctx = ("z", "y", "core")
    placed = (P(ctx, "tp"), P(ctx, "tp"), P(ctx, "tp"), P(), P(), P(ctx, "tp"))
    return jax.shard_map(
        on_device, mesh=split, in_specs=placed, out_specs=P(ctx, "tp"), check_vma=False
    )
```

```python
import functools
import math

import jax
import jax.numpy as jnp
from jax import lax
from jax.experimental import pallas as pl
from jax.experimental.pallas import tpu as pltpu
from jax.sharding import Mesh
from jax.sharding import PartitionSpec as P

HEAD = 128
BLOCK = 128
NEG = -1e30
BF16 = jnp.bfloat16
F32 = jnp.float32
NZ, NY, NC, NX = 8, 4, 2, 4
ROW = NY * NC
CTX = NZ * ROW
CHIPS = NZ * NY
REACH = 4
KEYS = 2 * (REACH + 1) * BLOCK
PROJECT_VMEM = 52
OFFSETS = [0, 1, 2, 3, 4, -1, -2, -3]
CHUNKS = [(0, 1, NY - 1), (2,)]


def fetch(copies):
    for copy in copies:
        copy.start()
    for copy in copies:
        copy.wait()


def join_kernel(k_ref, v_ref, o_ref, sems):
    width = k_ref.shape[1]
    fetch(
        [
            pltpu.make_async_copy(ref, o_ref.at[:, n * width : (n + 1) * width], sems.at[n])
            for n, ref in enumerate((k_ref, v_ref))
        ]
    )


def prepare_kernel(place_ref, homes_ref, ends_ref, q_ref, keep_ref, give_ref, bias_ref):
    index, core = place_ref[0], place_ref[1]
    swapped = index + 1 - 2 * core
    rows = lax.broadcasted_iota(jnp.int32, (BLOCK, BLOCK), 0)
    lanes = lax.broadcasted_iota(jnp.int32, (BLOCK, BLOCK), 1)
    parity = lanes % 2 == rows // CHIPS % 2
    half = rows // CTX
    own, other = homes_ref[0:1, :], homes_ref[1:2, :]

    select = (own == rows % CHIPS * NC + (half + core) % NC) & parity
    queries = jnp.dot(
        jnp.where(select, 1.0, 0.0).astype(BF16), q_ref[...], preferred_element_type=F32
    ).astype(BF16)
    keep_ref[...] = queries[:CTX]
    give_ref[...] = queries[CTX:]

    attended = (jnp.where(half == 0, own, other) == rows % CHIPS * NC + core) & parity
    token = jnp.sum(jnp.where(attended, lanes, 0), axis=1, keepdims=True)
    query_pos = jnp.where(half[:, :1] == 0, index, swapped) * BLOCK + token
    ends = ends_ref[...]
    doc_start = jnp.max(jnp.where(ends <= query_pos, ends, 0), axis=1, keepdims=True)
    blocks = [start - 2 * s for start in (index, swapped) for s in range(REACH + 1)]
    for n, block in enumerate(blocks):
        key_pos = block * BLOCK + lanes
        admitted = (key_pos <= query_pos) & (key_pos >= doc_start)
        bias_ref[:, n * BLOCK : (n + 1) * BLOCK] = jnp.where(admitted, 0.0, NEG)


def attend_kernel(bias_ref, keep_ref, got_ref, *refs):
    blocks, out_ref = refs[:-1], refs[-1]
    kv_heads = blocks[0].shape[1] // HEAD // 2
    group = keep_ref.shape[1] // HEAD // kv_heads

    scale = math.log2(math.e) / math.sqrt(HEAD)
    step = 2
    bias = jnp.concatenate([bias_ref[...]] * step, axis=0)
    for k in range(kv_heads):
        keys, values = [
            jnp.concatenate([ref[:, n * HEAD : (n + 1) * HEAD] for ref in blocks], axis=0)
            for n in (k, kv_heads + k)
        ]
        for g in range(0, group, step):
            columns = [(k * group + g + n) * HEAD for n in range(step)]
            stacked = jnp.concatenate(
                [ref[:, c : c + HEAD] for c in columns for ref in (keep_ref, got_ref)], axis=0
            )
            scores = lax.dot_general(
                stacked, keys, (((1,), (1,)), ((), ())), preferred_element_type=F32
            )
            scores = scores + bias
            top = jnp.max(scores, axis=1, keepdims=True)
            weights = jnp.exp2((scores - top) * scale)
            total = jnp.sum(weights, axis=1, keepdims=True)
            summed = jnp.dot(weights.astype(BF16), values, preferred_element_type=F32)
            attended = (summed / total).astype(BF16)
            for n, c in enumerate(columns):
                out_ref[:, c : c + HEAD] = attended[n * BLOCK : (n + 1) * BLOCK]


def sort_kernel(place_ref, *refs):
    *refs, sems = refs
    count = NC * len(OFFSETS)
    pieces, blocks, outs, sorted_ref = refs[:count], refs[count : -NX - 1], refs[-NX - 1 : -1], refs[-1]
    z, x, core = place_ref[0], place_ref[1], place_ref[2]
    rows = pieces[0].shape[0]
    copies = []
    for n, piece in enumerate(pieces):
        side, offset = n // len(OFFSETS), OFFSETS[n % len(OFFSETS)]
        source = (z + offset + NZ) % NZ
        row = pl.multiple_of(source % 2 * 128 + (core + side) % NC * rows, rows)
        target = sorted_ref.at[(source // 2 - x + NX) % NX, pl.ds(row, rows), :]
        copies.append(pltpu.make_async_copy(piece, target, sems.at[n]))
    fetch(copies)
    project_kernel(sorted_ref, *blocks, *outs)


def again_kernel(sorted_ref, *refs):
    *refs, held_ref, sems = refs
    copies = [
        pltpu.make_async_copy(sorted_ref.at[n], held_ref.at[n], sems.at[n]) for n in range(NX)
    ]
    for copy in copies:
        copy.start()
    project_kernel(held_ref, *refs, copies=copies)


def project_kernel(sorted_ref, *refs, copies=()):
    blocks, outs = refs[:-NX], refs[-NX:]
    attended = jnp.concatenate([ref[...] for ref in blocks], axis=0)
    for n, out in enumerate(outs):
        if copies:
            copies[n].wait()
        out[...] = lax.dot_general(
            attended, sorted_ref[n], (((1,), (1,)), ((), ())), preferred_element_type=F32
        ).astype(out.dtype)


def reduce_kernel(place_ref, *refs):
    shares, o_ref, total = refs[:-2], refs[-2], refs[-1]
    y, core = place_ref[0], place_ref[1]
    for chunk, sources in enumerate(CHUNKS):
        summed = shares[NX * chunk][...]
        for n in range(1, NX):
            summed = summed + shares[NX * chunk + n][...].astype(F32)
        for n in range(len(sources) * NC):
            row = ((y + sources[n // NC]) % NY * NC + (core + n) % NC) * CTX
            for half in range(2):
                total[half, pl.ds(pl.multiple_of(row, CTX), CTX), :] = summed[
                    n * CTX : (n + 1) * CTX, half * 128 : half * 128 + 128
                ]
    for half in range(2):
        for chip in range(CHIPS):
            o_ref[chip, :, half * 128 : half * 128 + 128] = total[
                half, pl.ds(chip, 16, stride=CHIPS), :
            ].astype(BF16)


def place_kernel(x_ref, o_ref):
    for z in range(NZ):
        for y in range(NY):
            for half in range(2):
                column = half * 512 + y * 128
                o_ref[z * 16 : z * 16 + 16, column : column + 128] = x_ref[
                    z * NY + y, :, half * 128 : half * 128 + 128
                ]


def call(kernel, out_shape, flops, moved, vmem=16, **kwargs):
    return pl.pallas_call(
        kernel,
        out_shape=out_shape,
        cost_estimate=pl.CostEstimate(flops=flops, bytes_accessed=moved, transcendentals=0),
        compiler_params=pltpu.CompilerParams(vmem_limit_bytes=vmem << 20),
        **kwargs,
    )


def chip_shift(value, steps):
    pairs = [
        (chip * NC + core, (chip + steps) % CHIPS * NC + core)
        for chip in range(CHIPS)
        for core in range(NC)
    ]
    return lax.ppermute(value, ("z", "y", "core"), pairs)


def ring_shift(value, axis, steps):
    count = lax.axis_size(axis)
    return lax.ppermute(value, axis, [(n, (n + steps) % count) for n in range(count)])


def core_swap(value):
    return lax.ppermute(value, "core", [(0, 1), (1, 0)])


def after(value, *earlier):
    return lax.optimization_barrier((value, *earlier))[0]


def on_device(queries, rotated_keys, value_vectors, doc_lengths, owner_lists, out_weight):
    index = lax.axis_index(("z", "y", "core")).astype(jnp.int32)
    at = {name: lax.axis_index(name).astype(jnp.int32) for name in ("z", "y", "core", "tp")}
    tokens, row_width = queries.shape
    vmem = pl.BlockSpec(memory_space=pltpu.VMEM)
    smem = pl.BlockSpec(memory_space=pltpu.SMEM)
    hbm = pl.BlockSpec(memory_space=pltpu.HBM)

    down = [out_weight]
    for _ in range(2):
        down.append(ring_shift(down[-1], "z", -1))

    own = call(
        join_kernel,
        jax.ShapeDtypeStruct((tokens, 2 * rotated_keys.shape[1]), BF16),
        0,
        1 << 18,
        in_specs=[hbm] * 2,
        out_specs=vmem,
        scratch_shapes=[pltpu.SemaphoreType.DMA((2,))],
    )(rotated_keys, value_vectors)
    mine = [own] + [chip_shift(own, s) for s in range(1, REACH + 1)]
    other = [core_swap(after(own, mine[1]))] + [core_swap(v) for v in mine[1:]]

    order = jnp.arange(doc_lengths.shape[0])
    ends = jnp.sum(jnp.where(order[None, :] <= order[:, None], doc_lengths[None, :], 0), axis=1)
    ends = jnp.pad(ends, (0, BLOCK - ends.shape[0]), constant_values=1 << 30).reshape(1, BLOCK)
    pair = lax.dynamic_slice_in_dim(owner_lists, index - at["core"], NC, axis=0)
    pair = jnp.where(at["core"] == 0, pair, pair[::-1])
    homes = jnp.broadcast_to(pair[:, :, None], (NC, CTX, tokens // CTX)).reshape(NC, tokens)
    half_rows = jax.ShapeDtypeStruct((tokens // 2, row_width), BF16)
    keep, give, bias = call(
        prepare_kernel,
        [half_rows, half_rows, jax.ShapeDtypeStruct((tokens, KEYS), F32)],
        2 * tokens * tokens * row_width,
        2 << 20,
        in_specs=[smem] + [vmem] * 3,
        out_specs=[vmem] * 3,
    )(
        jnp.stack([index, at["core"]]),
        homes.astype(jnp.int32),
        ends.astype(jnp.int32),
        after(queries, mine[1]),
    )
    attended = call(
        attend_kernel,
        jax.ShapeDtypeStruct((tokens, row_width), BF16),
        4 * tokens * row_width * KEYS,
        8 << 20,
        in_specs=[vmem] * (3 + 2 * (REACH + 1)),
        out_specs=vmem,
    )(bias, keep, core_swap(give), *mine, *other)
    rows = {0: attended} | {d: ring_shift(attended, "y", -d) for d in (1, 3)}
    for _ in range(2):
        down.append(ring_shift(down[-1], "z", -1))
    up = [after(out_weight, mine[1])]
    for _ in range(3):
        up.append(ring_shift(up[-1], "z", 1))
    middle = tokens // 2
    far = [rows[NY - 1][:middle], rows[1][middle:]]
    far = [ring_shift(far[0], "y", 1), ring_shift(far[1], "y", -1)]
    rows = {d: [block] for d, block in rows.items()} | {2: far}
    pieces = down + up[1:]
    pieces += [core_swap(after(piece, attended)) for piece in pieces]
    features = NZ * NC * out_weight.shape[0]
    corner = jnp.stack([at["z"], at["tp"], at["core"]])

    shares, weight = [], None
    for chunk in CHUNKS:
        blocks = [block for d in chunk for block in rows[d]]
        count = sum(block.shape[0] for block in blocks)
        shape = (count, features // NX)
        out_shapes = [jax.ShapeDtypeStruct(shape, F32)] + [jax.ShapeDtypeStruct(shape, BF16)] * 3
        flops = 2 * count * features * row_width
        if weight is None:
            *parts, weight = call(
                sort_kernel,
                out_shapes + [jax.ShapeDtypeStruct((NX, features // NX, row_width), BF16)],
                flops,
                8 << 20,
                vmem=PROJECT_VMEM,
                in_specs=[smem] + [hbm] * len(pieces) + [vmem] * len(blocks),
                out_specs=[vmem] * (NX + 1),
                scratch_shapes=[pltpu.SemaphoreType.DMA((len(pieces),))],
            )(corner, *pieces, *blocks)
        else:
            parts = call(
                again_kernel,
                out_shapes,
                flops,
                6 << 20,
                vmem=PROJECT_VMEM,
                in_specs=[hbm] + [vmem] * len(blocks),
                out_specs=[vmem] * NX,
                scratch_shapes=[
                    pltpu.VMEM(weight.shape, BF16),
                    pltpu.SemaphoreType.DMA((NX,)),
                ],
            )(weight, *blocks)
        shares += [parts[0]] + [ring_shift(parts[d], "tp", d) for d in (1, 3, 2)]

    sent = call(
        reduce_kernel,
        jax.ShapeDtypeStruct((CHIPS, 16, features // NX), BF16),
        4 << 20,
        2 << 20,
        in_specs=[smem] + [vmem] * len(shares),
        out_specs=vmem,
        scratch_shapes=[pltpu.VMEM((2, ROW * CTX, 128), F32)],
    )(jnp.stack([at["y"], at["core"]]), *shares)
    received = lax.all_to_all(sent, ("z", "y"), 0, 0, tiled=True)
    return call(
        place_kernel,
        jax.ShapeDtypeStruct((tokens, features), BF16),
        1 << 20,
        1 << 19,
        in_specs=[vmem],
        out_specs=vmem,
    )(received)


def solution(mesh):
    split = Mesh(mesh.devices.reshape(NZ, NY, NC, NX), ("z", "y", "core", "tp"))
    ctx = ("z", "y", "core")
    placed = (P(ctx, "tp"), P(ctx, "tp"), P(ctx, "tp"), P(), P(), P(ctx, "tp"))
    return jax.shard_map(
        on_device, mesh=split, in_specs=placed, out_specs=P(ctx, "tp"), check_vma=False
    )
```

```python
import functools
import math

import jax
import jax.numpy as jnp
from jax import lax
from jax.experimental import pallas as pl
from jax.experimental.pallas import tpu as pltpu
from jax.sharding import Mesh
from jax.sharding import PartitionSpec as P

HEAD = 128
BLOCK = 128
NEG = -1e30
BF16 = jnp.bfloat16
F32 = jnp.float32
NZ, NY, NC, NX = 8, 4, 2, 4
ROW = NY * NC
CTX = NZ * ROW
CHIPS = NZ * NY
REACH = 4
KEYS = 2 * (REACH + 1) * BLOCK
PROJECT_VMEM = 52
OFFSETS = [0, 1, 2, 3, 4, -1, -2, -3]
CHUNKS = [(0, 1, NY - 1), (2,)]


def fetch(copies):
    for copy in copies:
        copy.start()
    for copy in copies:
        copy.wait()


def join_kernel(k_ref, v_ref, o_ref, sems):
    width = k_ref.shape[1]
    fetch(
        [
            pltpu.make_async_copy(ref, o_ref.at[:, n * width : (n + 1) * width], sems.at[n])
            for n, ref in enumerate((k_ref, v_ref))
        ]
    )


def prepare_kernel(place_ref, homes_ref, ends_ref, q_ref, keep_ref, give_ref, bias_ref):
    index, core = place_ref[0], place_ref[1]
    swapped = index + 1 - 2 * core
    rows = lax.broadcasted_iota(jnp.int32, (BLOCK, BLOCK), 0)
    lanes = lax.broadcasted_iota(jnp.int32, (BLOCK, BLOCK), 1)
    parity = lanes % 2 == rows // CHIPS % 2
    half = rows // CTX
    own, other = homes_ref[0:1, :], homes_ref[1:2, :]

    select = (own == rows % CHIPS * NC + (half + core) % NC) & parity
    queries = jnp.dot(
        jnp.where(select, 1.0, 0.0).astype(BF16), q_ref[...], preferred_element_type=F32
    ).astype(BF16)
    keep_ref[...] = queries[:CTX]
    give_ref[...] = queries[CTX:]

    attended = (jnp.where(half == 0, own, other) == rows % CHIPS * NC + core) & parity
    token = jnp.sum(jnp.where(attended, lanes, 0), axis=1, keepdims=True)
    query_pos = jnp.where(half[:, :1] == 0, index, swapped) * BLOCK + token
    ends = ends_ref[...]
    doc_start = jnp.max(jnp.where(ends <= query_pos, ends, 0), axis=1, keepdims=True)
    blocks = [start - 2 * s for start in (index, swapped) for s in range(REACH + 1)]
    for n, block in enumerate(blocks):
        key_pos = block * BLOCK + lanes
        admitted = (key_pos <= query_pos) & (key_pos >= doc_start)
        bias_ref[:, n * BLOCK : (n + 1) * BLOCK] = jnp.where(admitted, 0.0, NEG)


def attend_kernel(bias_ref, keep_ref, got_ref, *refs):
    blocks, out_ref = refs[:-1], refs[-1]
    kv_heads = blocks[0].shape[1] // HEAD // 2
    group = keep_ref.shape[1] // HEAD // kv_heads

    scale = math.log2(math.e) / math.sqrt(HEAD)
    step = 2
    bias = jnp.concatenate([bias_ref[...]] * step, axis=0)
    for k in range(kv_heads):
        keys, values = [
            jnp.concatenate([ref[:, n * HEAD : (n + 1) * HEAD] for ref in blocks], axis=0)
            for n in (k, kv_heads + k)
        ]
        for g in range(0, group, step):
            columns = [(k * group + g + n) * HEAD for n in range(step)]
            stacked = jnp.concatenate(
                [ref[:, c : c + HEAD] for c in columns for ref in (keep_ref, got_ref)], axis=0
            )
            scores = lax.dot_general(
                stacked, keys, (((1,), (1,)), ((), ())), preferred_element_type=F32
            )
            scores = scores + bias
            top = jnp.max(scores, axis=1, keepdims=True)
            weights = jnp.exp2((scores - top) * scale)
            total = jnp.sum(weights, axis=1, keepdims=True)
            summed = jnp.dot(weights.astype(BF16), values, preferred_element_type=F32)
            attended = (summed / total).astype(BF16)
            for n, c in enumerate(columns):
                out_ref[:, c : c + HEAD] = attended[n * BLOCK : (n + 1) * BLOCK]


def sort_kernel(place_ref, *refs):
    *refs, sems = refs
    count = NC * len(OFFSETS)
    pieces, blocks, outs, sorted_ref = refs[:count], refs[count : -NX - 1], refs[-NX - 1 : -1], refs[-1]
    z, x, core = place_ref[0], place_ref[1], place_ref[2]
    rows = pieces[0].shape[0]
    copies = []
    for n, piece in enumerate(pieces):
        side, offset = n // len(OFFSETS), OFFSETS[n % len(OFFSETS)]
        source = (z + offset + NZ) % NZ
        row = pl.multiple_of(source % 2 * 128 + (core + side) % NC * rows, rows)
        target = sorted_ref.at[(source // 2 - x + NX) % NX, pl.ds(row, rows), :]
        copies.append(pltpu.make_async_copy(piece, target, sems.at[n]))
    fetch(copies)
    project_kernel(sorted_ref, *blocks, *outs)


def again_kernel(sorted_ref, *refs):
    *refs, held_ref, sems = refs
    copies = [
        pltpu.make_async_copy(sorted_ref.at[n], held_ref.at[n], sems.at[n]) for n in range(NX)
    ]
    for copy in copies:
        copy.start()
    project_kernel(held_ref, *refs, copies=copies)


def project_kernel(sorted_ref, *refs, copies=()):
    blocks, outs = refs[:-NX], refs[-NX:]
    attended = jnp.concatenate([ref[...] for ref in blocks], axis=0)
    for n, out in enumerate(outs):
        if copies:
            copies[n].wait()
        out[...] = lax.dot_general(
            attended, sorted_ref[n], (((1,), (1,)), ((), ())), preferred_element_type=F32
        ).astype(out.dtype)


def reduce_kernel(place_ref, *refs):
    shares, o_ref, total = refs[:-2], refs[-2], refs[-1]
    y, core = place_ref[0], place_ref[1]
    for chunk, sources in enumerate(CHUNKS):
        summed = shares[NX * chunk][...]
        for n in range(1, NX):
            summed = summed + shares[NX * chunk + n][...].astype(F32)
        for n in range(len(sources) * NC):
            row = ((y + sources[n // NC]) % NY * NC + (core + n) % NC) * CTX
            for half in range(2):
                total[half, pl.ds(pl.multiple_of(row, CTX), CTX), :] = summed[
                    n * CTX : (n + 1) * CTX, half * 128 : half * 128 + 128
                ]
    for half in range(2):
        for chip in range(CHIPS):
            o_ref[chip, :, half * 128 : half * 128 + 128] = total[
                half, pl.ds(chip, 16, stride=CHIPS), :
            ].astype(BF16)


def place_kernel(x_ref, o_ref):
    for z in range(NZ):
        for y in range(NY):
            for half in range(2):
                column = half * 512 + y * 128
                o_ref[z * 16 : z * 16 + 16, column : column + 128] = x_ref[
                    z * NY + y, :, half * 128 : half * 128 + 128
                ]


def call(kernel, out_shape, flops, moved, vmem=16, **kwargs):
    return pl.pallas_call(
        kernel,
        out_shape=out_shape,
        cost_estimate=pl.CostEstimate(flops=flops, bytes_accessed=moved, transcendentals=0),
        compiler_params=pltpu.CompilerParams(vmem_limit_bytes=vmem << 20),
        **kwargs,
    )


def chip_shift(value, steps):
    pairs = [
        (chip * NC + core, (chip + steps) % CHIPS * NC + core)
        for chip in range(CHIPS)
        for core in range(NC)
    ]
    return lax.ppermute(value, ("z", "y", "core"), pairs)


def ring_shift(value, axis, steps):
    count = lax.axis_size(axis)
    return lax.ppermute(value, axis, [(n, (n + steps) % count) for n in range(count)])


def core_swap(value):
    return lax.ppermute(value, "core", [(0, 1), (1, 0)])


def after(value, *earlier):
    return lax.optimization_barrier((value, *earlier))[0]


def on_device(queries, rotated_keys, value_vectors, doc_lengths, owner_lists, out_weight):
    index = lax.axis_index(("z", "y", "core")).astype(jnp.int32)
    at = {name: lax.axis_index(name).astype(jnp.int32) for name in ("z", "y", "core", "tp")}
    tokens, row_width = queries.shape
    vmem = pl.BlockSpec(memory_space=pltpu.VMEM)
    smem = pl.BlockSpec(memory_space=pltpu.SMEM)
    hbm = pl.BlockSpec(memory_space=pltpu.HBM)

    down = [out_weight]
    for _ in range(2):
        down.append(ring_shift(down[-1], "z", -1))

    own = call(
        join_kernel,
        jax.ShapeDtypeStruct((tokens, 2 * rotated_keys.shape[1]), BF16),
        0,
        1 << 18,
        vmem=PROJECT_VMEM,
        in_specs=[hbm] * 2,
        out_specs=vmem,
        scratch_shapes=[pltpu.SemaphoreType.DMA((2,))],
    )(rotated_keys, value_vectors)
    mine = [own] + [chip_shift(own, s) for s in range(1, REACH + 1)]
    other = [core_swap(after(own, mine[1]))] + [core_swap(v) for v in mine[1:]]

    order = jnp.arange(doc_lengths.shape[0])
    ends = jnp.sum(jnp.where(order[None, :] <= order[:, None], doc_lengths[None, :], 0), axis=1)
    ends = jnp.pad(ends, (0, BLOCK - ends.shape[0]), constant_values=1 << 30).reshape(1, BLOCK)
    pair = lax.dynamic_slice_in_dim(owner_lists, index - at["core"], NC, axis=0)
    pair = jnp.where(at["core"] == 0, pair, pair[::-1])
    homes = jnp.broadcast_to(pair[:, :, None], (NC, CTX, tokens // CTX)).reshape(NC, tokens)
    half_rows = jax.ShapeDtypeStruct((tokens // 2, row_width), BF16)
    keep, give, bias = call(
        prepare_kernel,
        [half_rows, half_rows, jax.ShapeDtypeStruct((tokens, KEYS), F32)],
        2 * tokens * tokens * row_width,
        2 << 20,
        in_specs=[smem] + [vmem] * 3,
        out_specs=[vmem] * 3,
    )(
        jnp.stack([index, at["core"]]),
        homes.astype(jnp.int32),
        ends.astype(jnp.int32),
        after(queries, mine[1]),
    )
    attended = call(
        attend_kernel,
        jax.ShapeDtypeStruct((tokens, row_width), BF16),
        4 * tokens * row_width * KEYS,
        8 << 20,
        in_specs=[vmem] * (3 + 2 * (REACH + 1)),
        out_specs=vmem,
    )(bias, keep, core_swap(give), *mine, *other)
    rows = {0: attended} | {d: ring_shift(attended, "y", -d) for d in (1, 3)}
    for _ in range(2):
        down.append(ring_shift(down[-1], "z", -1))
    up = [after(out_weight, mine[1])]
    for _ in range(3):
        up.append(ring_shift(up[-1], "z", 1))
    middle = tokens // 2
    far = [rows[NY - 1][:middle], rows[1][middle:]]
    far = [ring_shift(far[0], "y", 1), ring_shift(far[1], "y", -1)]
    rows = {d: [block] for d, block in rows.items()} | {2: far}
    pieces = down + up[1:]
    pieces += [core_swap(after(piece, attended)) for piece in pieces]
    features = NZ * NC * out_weight.shape[0]
    corner = jnp.stack([at["z"], at["tp"], at["core"]])

    shares, weight = [], None
    for chunk in CHUNKS:
        blocks = [block for d in chunk for block in rows[d]]
        count = sum(block.shape[0] for block in blocks)
        shape = (count, features // NX)
        out_shapes = [jax.ShapeDtypeStruct(shape, F32)] + [jax.ShapeDtypeStruct(shape, BF16)] * 3
        flops = 2 * count * features * row_width
        if weight is None:
            *parts, weight = call(
                sort_kernel,
                out_shapes + [jax.ShapeDtypeStruct((NX, features // NX, row_width), BF16)],
                flops,
                8 << 20,
                vmem=PROJECT_VMEM,
                in_specs=[smem] + [hbm] * len(pieces) + [vmem] * len(blocks),
                out_specs=[vmem] * (NX + 1),
                scratch_shapes=[pltpu.SemaphoreType.DMA((len(pieces),))],
            )(corner, *pieces, *blocks)
        else:
            parts = call(
                again_kernel,
                out_shapes,
                flops,
                6 << 20,
                vmem=PROJECT_VMEM,
                in_specs=[hbm] + [vmem] * len(blocks),
                out_specs=[vmem] * NX,
                scratch_shapes=[
                    pltpu.VMEM(weight.shape, BF16),
                    pltpu.SemaphoreType.DMA((NX,)),
                ],
            )(weight, *blocks)
        shares += [parts[0]] + [ring_shift(parts[d], "tp", d) for d in (1, 3, 2)]

    sent = call(
        reduce_kernel,
        jax.ShapeDtypeStruct((CHIPS, 16, features // NX), BF16),
        4 << 20,
        2 << 20,
        in_specs=[smem] + [vmem] * len(shares),
        out_specs=vmem,
        scratch_shapes=[pltpu.VMEM((2, ROW * CTX, 128), F32)],
    )(jnp.stack([at["y"], at["core"]]), *shares)
    received = lax.all_to_all(sent, ("z", "y"), 0, 0, tiled=True)
    return call(
        place_kernel,
        jax.ShapeDtypeStruct((tokens, features), BF16),
        1 << 20,
        1 << 19,
        in_specs=[vmem],
        out_specs=vmem,
    )(received)


def solution(mesh):
    split = Mesh(mesh.devices.reshape(NZ, NY, NC, NX), ("z", "y", "core", "tp"))
    ctx = ("z", "y", "core")
    placed = (P(ctx, "tp"), P(ctx, "tp"), P(ctx, "tp"), P(), P(), P(ctx, "tp"))
    return jax.shard_map(
        on_device, mesh=split, in_specs=placed, out_specs=P(ctx, "tp"), check_vma=False
    )
```
